768 devices in a mesh: grp: 32 (over x, y), sec: 24 (over z, core).
Axes of the slice: x: 4, y: 8, z: 12, core: 2. Of those that a mesh axis runs over, the one named last changes fastest.
Arguments:
- wavefunction: bfloat16 [512, 96, 512], P('grp', 'sec'), may hold values from -6 to 6
- left_ops: bfloat16 [3072, 512, 512], P(('grp', 'sec')), may hold values from -0.25 to 0.25
- right_ops: bfloat16 [3072, 512, 512], P(('grp', 'sec')), may hold values from -0.046875 to 0.046875
- in_sector: int32 [3072], P(('grp', 'sec')), may hold values from 0 to 3
- out_sector: int32 [3072], P(('grp', 'sec')), may hold values from 0 to 3
- term_count: int32 [768], P(('grp', 'sec')), may hold values from 1 to 4
Outputs:
- sigma_block: bfloat16 [512, 96, 512], P('grp', 'sec')
The draws below stay inside these ranges and needn't reach their ends.
Inputs may be any that keep to these rules, and one draw needn't show every extreme that they name: `term_count`: each device has between 1 and 4 live slots; its live slots come first.
All inputs are finite; a program needn't handle non-finite values.
Results may differ from the reference program's by a relative error of at most 0.0049.
Values may be sent and summed in bfloat16 or wider, within the bound.
A program may use at most 32 MiB of HBM per device.

```python
import jax
import jax.numpy as jnp
from jax import lax

B = 512
SEC_COL = 4
TSLOT = 4
S = 96
SLOTS = 3072
N_GRP = 32
N_SEC = 24


def with_ends(array, own_key, smallest, top_value):
    longest = array.shape.index(max(array.shape))
    spots = []
    for shift in (0, 1):
        where = [jax.random.randint(jax.random.fold_in(own_key, axis), (), 0, length) for axis, length in enumerate(array.shape)]
        where[longest] = (where[longest] + shift) % array.shape[longest]
        spots.append(tuple(where))
    return array.at[spots[0]].set(smallest).at[spots[1]].set(top_value)


def level_of(key, extent, pieces, least, largest):
    def one(dim, parts):
        steps = jax.random.uniform(jax.random.fold_in(jax.random.fold_in(key, 6), dim), (parts,), jnp.float32, least / len(pieces), largest / len(pieces))
        return jnp.repeat(jnp.exp(steps), extent[dim] // parts).reshape((-1,) + (1,) * (len(extent) - dim - 1))

    level = one(*pieces[0])
    for cut in pieces[1:]:
        level = level * one(*cut)
    return level


def normal_values(key, shape, width, reach, split=(), kind=jnp.bfloat16):
    gain = level_of(key, shape, split, -0.22, 0.18) if split else 1.0
    array = jax.random.normal(key, shape, jnp.float32) * width * gain
    return jnp.minimum(jnp.maximum(array, -reach), reach).astype(kind)


def setup_inputs(seed: int = 0) -> dict:
    splits = jax.random.split(jax.random.key(seed), 7)
    return {
        "wavefunction": normal_values(splits[0], (B, S, B), 1.0, 6.0, ((0, 32), (1, 24))),
        "left_ops": normal_values(splits[1], (SLOTS, B, B), B ** -0.5, 0.25, ((0, 768),)),
        "right_ops": normal_values(splits[2], (SLOTS, B, B), (B * N_GRP) ** -0.5, 0.046875, ((0, 768),)),
        "in_sector": with_ends(jax.random.randint(splits[3], (SLOTS,), 0, SEC_COL), jax.random.fold_in(splits[3], 1), 0, SEC_COL - 1).astype(jnp.int32),
        "out_sector": with_ends(jax.random.randint(splits[4], (SLOTS,), 0, SEC_COL), jax.random.fold_in(splits[4], 1), 0, SEC_COL - 1).astype(jnp.int32),
        "term_count": with_ends(jax.random.randint(splits[5], (N_GRP * N_SEC,), 1, TSLOT + 1), jax.random.fold_in(splits[5], 1), 1, TSLOT).astype(jnp.int32),
    }


def reference(wavefunction, left_ops, right_ops, in_sector, out_sector, term_count):
    def absorb_slot(running, slot_index):
        column = (slot_index // TSLOT) % N_SEC
        source = (column * SEC_COL + in_sector[slot_index]).astype(jnp.int32)
        target = (column * SEC_COL + out_sector[slot_index]).astype(jnp.int32)
        active = ((slot_index % TSLOT) < term_count[slot_index // TSLOT]).astype(jnp.float32)
        chosen = lax.dynamic_index_in_dim(wavefunction, source, 1, keepdims=False)
        product = jnp.dot(left_ops[slot_index], chosen, preferred_element_type=jnp.float32).astype(jnp.bfloat16)
        projected = jnp.dot(product, right_ops[slot_index].T, preferred_element_type=jnp.float32) * active
        current = lax.dynamic_index_in_dim(running, target, 1, keepdims=False)
        running = lax.dynamic_update_index_in_dim(running, current + projected, target, 1)
        return running, None

    start_sum = jnp.zeros((B, S, B), jnp.float32)
    final_sum, unused = lax.scan(absorb_slot, start_sum, jnp.arange(SLOTS, dtype=jnp.int32))
    return final_sum.astype(jnp.bfloat16)
```

```python
import jax
import jax.numpy as jnp
from jax import lax
from jax.experimental import pallas as pl
from jax.experimental.pallas import tpu as pltpu
from jax.sharding import PartitionSpec as P

NX, NY = 4, 8
MESH = pl.DeviceIdType.MESH


def kernel(
    in_ref, out_ref, count_ref, own_ref, left_hbm, right_hbm, o_ref,
    state, left, right, prod, part, fbuf,
    y_send, y_recv, x_send, x_recv,
    load_sem, agx_ss, agx_rs, agy_ss, agy_rs, rsy_ss, rsy_rs, rsx_ss, rsx_rs,
):
    g = lax.axis_index("grp")
    x, y = g // NY, lax.rem(g, NY)
    half = o_ref.shape[2] // 2

    def dev(dx, dy):
        return {"grp": lax.rem(x + dx + NX, NX) * NY + lax.rem(y + dy + NY, NY)}

    loads = [
        pltpu.make_async_copy(left_hbm, left, load_sem.at[0]),
        pltpu.make_async_copy(right_hbm, right, load_sem.at[1]),
        pltpu.make_async_copy(own_ref, state.at[x, y], load_sem.at[2]),
    ]
    for load in loads:
        load.start()

    barrier = pltpu.get_barrier_semaphore()
    peers = [(1, 0), (2, 0), (3, 0), (0, 1), (0, -1)]
    for dx, dy in peers:
        pl.semaphore_signal(barrier, inc=1, device_id=dev(dx, dy), device_id_type=MESH)
    pl.semaphore_wait(barrier, len(peers))

    started = []

    def remote(src, dst, ss, rs, where):
        copy = pltpu.make_async_remote_copy(
            src_ref=src, dst_ref=dst, send_sem=ss, recv_sem=rs, device_id=where, device_id_type=MESH
        )
        copy.start()
        started.append(copy)
        return copy

    gx = [
        remote(own_ref, state.at[x, y], agx_ss.at[j - 1], agx_rs.at[j - 1], dev(j, 0))
        for j in (1, 3, 2)
    ]
    loads[2].wait()
    for copy in gx:
        copy.wait_recv()

    def ring(k, h, d):
        block = lax.rem(y - d * (k - 1) + NY, NY)
        piece = state.at[2 * h:2 * h + 2, block]
        i = (1 - d) // 2
        return remote(piece, piece, agy_ss.at[i, k - 1, h], agy_rs.at[i, k - 1, h], dev(0, d))

    held = {}
    for k in range(1, 5):
        for h in range(2):
            for d in (1, -1):
                if k > 1:
                    held[k - 1, h, d].wait_recv()
                if k < 4 or (h == 0) == (d == 1):
                    held[k, h, d] = ring(k, h, d)
    held[4, 0, 1].wait_recv()
    held[4, 1, -1].wait_recv()

    loads[0].wait()
    rows = NX * NY * own_ref.shape[1]

    def first(q, carry):
        block = state[:, :, in_ref[q]].reshape(rows, 2 * half)
        for m in range(2):
            span = slice(m * (rows // 2), (m + 1) * (rows // 2))
            prod[q, span] = jnp.dot(
                left[q, span], block, preferred_element_type=jnp.float32
            ).astype(jnp.bfloat16)
        return carry

    lax.fori_loop(0, 4, first, 0)
    loads[1].wait()

    weight = [
        [
            jnp.where((out_ref[q] == t) & (q < count_ref[0]), jnp.float32(1), jnp.float32(0))
            for t in range(4)
        ]
        for q in range(4)
    ]

    def second(c, h):
        span = slice(h * (rows // 2), (h + 1) * (rows // 2))
        proj = [
            lax.dot_general(
                prod[q, span], right[q, c * half:(c + 1) * half],
                (((1,), (1,)), ((), ())), preferred_element_type=jnp.float32,
            )
            for q in range(4)
        ]
        for t in range(4):
            total = proj[0] * weight[0][t]
            for q in range(1, 4):
                total = total + proj[q] * weight[q][t]
            part[c, 2 * h:2 * h + 2, :, t] = total.reshape(2, NY, own_ref.shape[1], half)

    def scatter(c):
        got = {}

        def step(k, h, d):
            i = (1 - d) // 2
            value = part[c, 2 * h:2 * h + 2, lax.rem(y + d * k + NY, NY)]
            if (k + 1, h, d) in got:
                got[k + 1, h, d].wait_recv()
                value = value + y_recv[c, i, k, h].astype(jnp.float32)
            y_send[c, i, k - 1, h] = value.astype(jnp.bfloat16)
            got[k, h, d] = remote(
                y_send.at[c, i, k - 1, h], y_recv.at[c, i, k - 1, h],
                rsy_ss.at[c, i, k - 1, h], rsy_rs.at[c, i, k - 1, h], dev(0, d),
            )

        step(4, 0, 1), step(4, 1, -1), step(3, 1, 1), step(3, 0, -1)
        yield
        step(3, 0, 1), step(3, 1, -1)
        yield
        for k in (2, 1):
            step(k, 1, 1), step(k, 0, -1)
            yield
            step(k, 0, 1), step(k, 1, -1)
            yield
        for h in (0, 1):
            value = part[c, 2 * h:2 * h + 2, y]
            for d in (1, -1):
                got[1, h, d].wait_recv()
                value = value + y_recv[c, (1 - d) // 2, 0, h].astype(jnp.float32)
            fbuf[c, 2 * h:2 * h + 2] = value
        cross = []
        for j in (2, 1, 3):
            x_send[c, j - 1] = fbuf[c, lax.rem(x + j, NX)].astype(jnp.bfloat16)
            cross.append(remote(
                x_send.at[c, j - 1], x_recv.at[c, j - 1],
                rsx_ss.at[c, j - 1], rsx_rs.at[c, j - 1], dev(j, 0),
            ))
        yield
        value = fbuf[c, x]
        for copy in cross:
            copy.wait_recv()
        for j in (1, 2, 3):
            value = value + x_recv[c, j - 1].astype(jnp.float32)
        o_ref[:, :, c * half:(c + 1) * half] = value.astype(jnp.bfloat16)

    second(0, 0)
    second(0, 1)
    flow0, flow1 = scatter(0), scatter(1)
    next(flow0)
    second(1, 0)
    next(flow0)
    second(1, 1)
    next(flow1)
    live = [flow0, flow1]
    while live:
        for flow in list(live):
            try:
                next(flow)
            except StopIteration:
                live.remove(flow)
    for copy in started:
        copy.wait_send()


def on_device(wavefunction, left_ops, right_ops, in_sector, out_sector, term_count):
    own = wavefunction.transpose(1, 0, 2)
    sectors, block, order = own.shape
    half = order // 2
    slots = left_ops.shape[0]
    vmem = pl.BlockSpec(memory_space=pltpu.VMEM)
    smem = pl.BlockSpec(memory_space=pltpu.SMEM)
    hbm = pl.BlockSpec(memory_space=pl.ANY)
    dma = pltpu.SemaphoreType.DMA
    result = pl.pallas_call(
        kernel,
        out_shape=jax.ShapeDtypeStruct((sectors, block, order), jnp.bfloat16),
        in_specs=[smem, smem, smem, vmem, hbm, hbm],
        out_specs=vmem,
        scratch_shapes=[
            pltpu.VMEM((NX, NY, sectors, block, order), jnp.bfloat16),
            pltpu.VMEM(left_ops.shape, jnp.bfloat16),
            pltpu.VMEM(right_ops.shape, jnp.bfloat16),
            pltpu.VMEM((slots, left_ops.shape[1], order), jnp.bfloat16),
            pltpu.VMEM((2, NX, NY, sectors, block, half), jnp.float32),
            pltpu.VMEM((2, NX, sectors, block, half), jnp.float32),
            pltpu.VMEM((2, 2, 4, 2, 2, sectors, block, half), jnp.bfloat16),
            pltpu.VMEM((2, 2, 4, 2, 2, sectors, block, half), jnp.bfloat16),
            pltpu.VMEM((2, 3, sectors, block, half), jnp.bfloat16),
            pltpu.VMEM((2, 3, sectors, block, half), jnp.bfloat16),
            dma((3,)),
            dma((3,)), dma((3,)),
            dma((2, 4, 2)), dma((2, 4, 2)),
            dma((2, 2, 4, 2)), dma((2, 2, 4, 2)),
            dma((2, 3)), dma((2, 3)),
        ],
        compiler_params=pltpu.CompilerParams(collective_id=0, has_side_effects=True),
        name="gather_apply_scatter",
    )(in_sector, out_sector, term_count, own, left_ops, right_ops)
    return result.transpose(1, 0, 2)


def solution(mesh):
    return jax.shard_map(
        on_device,
        mesh=mesh,
        in_specs=(
            P("grp", "sec", None),
            P(("grp", "sec"), None, None),
            P(("grp", "sec"), None, None),
            P(("grp", "sec")),
            P(("grp", "sec")),
            P(("grp", "sec")),
        ),
        out_specs=P("grp", "sec", None),
        check_vma=False,
    )
```

```python
import jax
import jax.numpy as jnp
from jax import lax
from jax.experimental import pallas as pl
from jax.experimental.pallas import tpu as pltpu
from jax.sharding import PartitionSpec as P

NX, NY = 4, 8
MESH = pl.DeviceIdType.MESH


def kernel(
    in_ref, out_ref, count_ref, own_ref, left_hbm, right_hbm, o_ref,
    state0, state1, left, right, prod, part, fbuf, gbuf,
    y_send, y_recv, x_send, x_recv, v_send, v_recv, u_send, u_recv,
    load_sem, agx_ss, agx_rs, agy_ss, agy_rs, agv_ss, agv_rs, agu_ss, agu_rs,
    rsy_ss, rsy_rs, rsx_ss, rsx_rs, rsv_ss, rsv_rs, rsu_ss, rsu_rs,
):
    g = lax.axis_index("grp")
    x, y = g // NY, lax.rem(g, NY)
    half = o_ref.shape[2] // 2

    def dev(dx, dy):
        return {"grp": lax.rem(x + dx + NX, NX) * NY + lax.rem(y + dy + NY, NY)}

    loads = [
        pltpu.make_async_copy(left_hbm, left, load_sem.at[0]),
        pltpu.make_async_copy(right_hbm, right, load_sem.at[1]),
        pltpu.make_async_copy(own_ref.at[0], state0.at[x, y], load_sem.at[2]),
        pltpu.make_async_copy(own_ref.at[1], state1.at[x, y], load_sem.at[3]),
    ]
    for load in loads:
        load.start()

    barrier = pltpu.get_barrier_semaphore()
    peers = [(1, 0), (2, 0), (3, 0), (0, 1), (0, -1)]
    for dx, dy in peers:
        pl.semaphore_signal(barrier, inc=1, device_id=dev(dx, dy), device_id_type=MESH)
    pl.semaphore_wait(barrier, len(peers))

    started = []

    def remote(src, dst, ss, rs, where):
        copy = pltpu.make_async_remote_copy(
            src_ref=src, dst_ref=dst, send_sem=ss, recv_sem=rs, device_id=where, device_id_type=MESH
        )
        copy.start()
        started.append(copy)
        return copy

    def ring(k, h, d):
        block = lax.rem(y - d * (k - 1) + NY, NY)
        piece = state0.at[2 * h:2 * h + 2, block]
        i = (1 - d) // 2
        return remote(piece, piece, agy_ss.at[i, k - 1, h], agy_rs.at[i, k - 1, h], dev(0, d))

    held = {}

    def ring_round(k):
        for h in range(2):
            for d in (1, -1):
                if k > 1:
                    held[k - 1, h, d].wait_recv()
                if k < 4 or (h == 0) == (d == 1):
                    held[k, h, d] = ring(k, h, d)

    passed, crossed, forwarded = {}, {}, {}
    blocks = [(0, 1), (1, 1), (1, -1), (2, 1), (2, -1), (3, 1), (3, -1), (4, 1)]

    def pass_on(k, d):
        i = (1 - d) // 2
        here = own_ref.at[1] if k == 1 else state1.at[x, lax.rem(y - d * (k - 1) + NY, NY)]
        there = state1.at[x, lax.rem(y - d * (k - 1) + NY, NY)]
        if k == 4:
            here, there = here.at[2 * i:2 * i + 2], there.at[2 * i:2 * i + 2]
        passed[k, d] = remote(here, there, agv_ss.at[i, k - 1], agv_rs.at[i, k - 1], dev(0, d))

    def cross(k, d):
        p = blocks.index((k, d))
        there = state1.at[x, lax.rem(y - d * k + NY, NY)]
        here = own_ref.at[1] if k == 0 else there
        for i in range(2):
            crossed[k, d, i] = remote(here, there, agu_ss.at[p, i], agu_rs.at[p, i], dev(1 - 2 * i, 0))

    def forward(k, d):
        p = blocks.index((k, d))
        way = {0: 1, 1: d, 2: -d, 3: d, 4: -1}[k]
        crossed[k, d, (1 - way) // 2].wait_recv()
        piece = state1.at[lax.rem(x - way + NX, NX), lax.rem(y - d * k + NY, NY)]
        forwarded[k, d] = remote(piece, piece, agu_ss.at[p, 2], agu_rs.at[p, 2], dev(way, 0))
        return crossed[k, d, (1 + way) // 2]

    gx = [
        remote(own_ref.at[0], state0.at[x, y], agx_ss.at[j - 1], agx_rs.at[j - 1], dev(j, 0))
        for j in (1, 3, 2)
    ]
    pass_on(1, 1), pass_on(1, -1), cross(0, 1)
    loads[2].wait()
    loads[3].wait()
    for copy in gx:
        copy.wait_recv()
    ring_round(1)
    rest = []
    before = [(0, 1)]
    for k in range(1, 5):
        for d in (1, -1):
            passed[k, d].wait_recv()
        for d in (1, -1):
            if k < 4:
                pass_on(k + 1, d)
        now = [(k, 1), (k, -1)] if k < 4 else [(4, 1)]
        for which in now:
            cross(*which)
        for which in before:
            rest.append(forward(*which))
        before = now
        if k < 4:
            ring_round(k + 1)
    held[4, 0, 1].wait_recv()
    held[4, 1, -1].wait_recv()

    loads[0].wait()
    rows = NX * NY * own_ref.shape[2]

    def first(q, c):
        block = (state0, state1)[c][:, :, in_ref[q]].reshape(rows, half)
        prod[q, :, c * half:(c + 1) * half] = jnp.dot(
            left[q], block, preferred_element_type=jnp.float32
        ).astype(jnp.bfloat16)

    first(0, 0)
    rest.append(forward(4, 1))
    for q in range(1, 4):
        first(q, 0)
    for copy in rest:
        copy.wait_recv()
    for copy in forwarded.values():
        copy.wait_recv()
    for q in range(4):
        first(q, 1)
    loads[1].wait()

    weight = [
        [
            jnp.where((out_ref[q] == t) & (q < count_ref[0]), jnp.float32(1), jnp.float32(0))
            for t in range(4)
        ]
        for q in range(4)
    ]

    def second(c, h):
        span = slice(h * (rows // 2), (h + 1) * (rows // 2))
        proj = [
            lax.dot_general(
                prod[q, span], right[q, c * half:(c + 1) * half],
                (((1,), (1,)), ((), ())), preferred_element_type=jnp.float32,
            )
            for q in range(4)
        ]
        for t in range(4):
            total = proj[0] * weight[0][t]
            for q in range(1, 4):
                total = total + proj[q] * weight[q][t]
            part[c, 2 * h:2 * h + 2, :, t] = total.reshape(2, NY, own_ref.shape[2], half)

    def scatter_y_x(c):
        got = {}

        def step(k, h, d):
            i = (1 - d) // 2
            value = part[c, 2 * h:2 * h + 2, lax.rem(y + d * k + NY, NY)]
            if (k + 1, h, d) in got:
                got[k + 1, h, d].wait_recv()
                value = value + y_recv[i, k, h].astype(jnp.float32)
            y_send[i, k - 1, h] = value.astype(jnp.bfloat16)
            got[k, h, d] = remote(
                y_send.at[i, k - 1, h], y_recv.at[i, k - 1, h],
                rsy_ss.at[i, k - 1, h], rsy_rs.at[i, k - 1, h], dev(0, d),
            )

        step(4, 0, 1), step(4, 1, -1), step(3, 1, 1), step(3, 0, -1)
        yield
        step(3, 0, 1), step(3, 1, -1)
        yield
        for k in (2, 1):
            step(k, 1, 1), step(k, 0, -1)
            yield
            step(k, 0, 1), step(k, 1, -1)
            yield
        for h in (0, 1):
            value = part[c, 2 * h:2 * h + 2, y]
            for d in (1, -1):
                got[1, h, d].wait_recv()
                value = value + y_recv[(1 - d) // 2, 0, h].astype(jnp.float32)
            fbuf[2 * h:2 * h + 2] = value
        cross = []
        for j in (2, 1, 3):
            x_send[j - 1] = fbuf[lax.rem(x + j, NX)].astype(jnp.bfloat16)
            cross.append(remote(
                x_send.at[j - 1], x_recv.at[j - 1],
                rsx_ss.at[j - 1], rsx_rs.at[j - 1], dev(j, 0),
            ))
        yield
        value = fbuf[x]
        for copy in cross:
            copy.wait_recv()
        for j in (1, 2, 3):
            value = value + x_recv[j - 1].astype(jnp.float32)
        o_ref[:, :, c * half:(c + 1) * half] = value.astype(jnp.bfloat16)

    groups = [(4, 3), (-3, 2), (-2, 1), (-1, 0)]

    def scatter_x_y(c):
        got = {}

        def block(dx, j):
            return part[c, lax.rem(x + dx + NX, NX), lax.rem(y + j + NY, NY)]

        def step(n, k, d):
            main = 1 - 2 * (n % 2)
            kind = 0 if k == 2 else (1 if d == main else 2)
            for m, j in enumerate(groups[n]):
                value = block(d * k, j)
                if kind == 1:
                    if m == 0:
                        got[n, 0].wait_recv()
                    value = value + u_recv[0, n, m].astype(jnp.float32)
                u_send[kind, n, m] = value.astype(jnp.bfloat16)
            got[n, kind] = remote(
                u_send.at[kind, n], u_recv.at[kind, n], rsu_ss.at[kind, n], rsu_rs.at[kind, n], dev(d, 0)
            )

        def settle(n):
            got[n, 1].wait_recv()
            got[n, 2].wait_recv()
            for m, j in enumerate(groups[n]):
                gbuf[j + 3] = (
                    block(0, j) + u_recv[1, n, m].astype(jnp.float32) + u_recv[2, n, m].astype(jnp.float32)
                )

        def pass_back(k, d):
            i = (1 - d) // 2
            value = gbuf[d * k + 3]
            if (d, k + 1) in got:
                got[d, k + 1].wait_recv()
                value = value + v_recv[i, k].astype(jnp.float32)
            v_send[i, k - 1] = value.astype(jnp.bfloat16)
            got[d, k] = remote(
                v_send.at[i, k - 1], v_recv.at[i, k - 1], rsv_ss.at[i, k - 1], rsv_rs.at[i, k - 1], dev(0, d)
            )

        step(0, 2, 1), step(1, 2, -1), step(2, 2, 1), step(3, 2, -1)
        step(0, 1, -1), step(1, 1, 1)
        yield
        step(0, 1, 1), step(1, 1, -1)
        step(2, 1, -1), step(3, 1, 1)
        yield
        step(2, 1, 1), step(3, 1, -1)
        yield
        settle(0)
        pass_back(4, 1)
        settle(1)
        pass_back(3, -1)
        yield
        settle(2)
        pass_back(3, 1), pass_back(2, -1)
        yield
        settle(3)
        pass_back(2, 1), pass_back(1, -1)
        yield
        pass_back(1, 1)
        yield
        value = gbuf[3]
        for i, d in ((0, 1), (1, -1)):
            got[d, 1].wait_recv()
            value = value + v_recv[i, 0].astype(jnp.float32)
        o_ref[:, :, c * half:(c + 1) * half] = value.astype(jnp.bfloat16)

    second(1, 0)
    second(1, 1)
    flow0, flow1 = scatter_y_x(0), scatter_x_y(1)
    next(flow1)
    second(0, 0)
    next(flow1)
    second(0, 1)
    next(flow0)
    live = [flow1, flow0]
    while live:
        for flow in list(live):
            try:
                next(flow)
            except StopIteration:
                live.remove(flow)
    for copy in started:
        copy.wait_send()


def on_device(wavefunction, left_ops, right_ops, in_sector, out_sector, term_count):
    block, sectors, order = wavefunction.shape
    half = order // 2
    own = wavefunction.reshape(block, sectors, 2, half).transpose(2, 1, 0, 3)
    slots = left_ops.shape[0]
    piece = (sectors, block, half)
    vmem = pl.BlockSpec(memory_space=pltpu.VMEM)
    smem = pl.BlockSpec(memory_space=pltpu.SMEM)
    hbm = pl.BlockSpec(memory_space=pl.ANY)
    dma = pltpu.SemaphoreType.DMA
    result = pl.pallas_call(
        kernel,
        out_shape=jax.ShapeDtypeStruct((sectors, block, order), jnp.bfloat16),
        in_specs=[smem, smem, smem, vmem, hbm, hbm],
        out_specs=vmem,
        scratch_shapes=[
            pltpu.VMEM((NX, NY, *piece), jnp.bfloat16),
            pltpu.VMEM((NX, NY, *piece), jnp.bfloat16),
            pltpu.VMEM(left_ops.shape, jnp.bfloat16),
            pltpu.VMEM(right_ops.shape, jnp.bfloat16),
            pltpu.VMEM((slots, left_ops.shape[1], order), jnp.bfloat16),
            pltpu.VMEM((2, NX, NY, *piece), jnp.float32),
            pltpu.VMEM((NX, *piece), jnp.float32),
            pltpu.VMEM((NY, *piece), jnp.float32),
            pltpu.VMEM((2, 4, 2, 2, *piece), jnp.bfloat16),
            pltpu.VMEM((2, 4, 2, 2, *piece), jnp.bfloat16),
            pltpu.VMEM((3, *piece), jnp.bfloat16),
            pltpu.VMEM((3, *piece), jnp.bfloat16),
            pltpu.VMEM((2, 4, *piece), jnp.bfloat16),
            pltpu.VMEM((2, 4, *piece), jnp.bfloat16),
            pltpu.VMEM((3, 4, 2, *piece), jnp.bfloat16),
            pltpu.VMEM((3, 4, 2, *piece), jnp.bfloat16),
            dma((4,)),
            dma((3,)), dma((3,)),
            dma((2, 4, 2)), dma((2, 4, 2)),
            dma((2, 4)), dma((2, 4)),
            dma((8, 3)), dma((8, 3)),
            dma((2, 4, 2)), dma((2, 4, 2)),
            dma((3,)), dma((3,)),
            dma((2, 4)), dma((2, 4)),
            dma((3, 4)), dma((3, 4)),
        ],
        compiler_params=pltpu.CompilerParams(collective_id=0, has_side_effects=True),
        name="gather_apply_scatter",
    )(in_sector, out_sector, term_count, own, left_ops, right_ops)
    return result.transpose(1, 0, 2)


def solution(mesh):
    return jax.shard_map(
        on_device,
        mesh=mesh,
        in_specs=(
            P("grp", "sec", None),
            P(("grp", "sec"), None, None),
            P(("grp", "sec"), None, None),
            P(("grp", "sec")),
            P(("grp", "sec")),
            P(("grp", "sec")),
        ),
        out_specs=P("grp", "sec", None),
        check_vma=False,
    )
```

```python
import jax
import jax.numpy as jnp
from jax import lax
from jax.experimental import pallas as pl
from jax.experimental.pallas import tpu as pltpu
from jax.sharding import PartitionSpec as P

NX, NY = 4, 8
MESH = pl.DeviceIdType.MESH


def kernel(
    in_ref, out_ref, count_ref, own_ref, left_hbm, right_hbm, o_ref,
    state0, state1, left, right, prod, part, fbuf, gbuf,
    y_send, y_recv, x_send, x_recv, v_send, v_recv, u_send, u_recv,
    load_sem, agx_ss, agx_rs, agy_ss, agy_rs, agv_ss, agv_rs, agu_ss, agu_rs,
    rsy_ss, rsy_rs, rsx_ss, rsx_rs, rsv_ss, rsv_rs, rsu_ss, rsu_rs,
):
    g = lax.axis_index("grp")
    x, y = g // NY, lax.rem(g, NY)
    half = o_ref.shape[2] // 2

    def dev(dx, dy):
        return {"grp": lax.rem(x + dx + NX, NX) * NY + lax.rem(y + dy + NY, NY)}

    loads = [
        pltpu.make_async_copy(left_hbm, left, load_sem.at[0]),
        pltpu.make_async_copy(right_hbm, right, load_sem.at[1]),
        pltpu.make_async_copy(own_ref.at[0], state0.at[x, y], load_sem.at[2]),
        pltpu.make_async_copy(own_ref.at[1], state1.at[x, y], load_sem.at[3]),
    ]
    for load in loads:
        load.start()

    barrier = pltpu.get_barrier_semaphore()
    peers = [(j, 0) for j in range(1, NX)] + [(0, j) for j in range(1, NY)]
    for dx, dy in peers:
        pl.semaphore_signal(barrier, inc=1, device_id=dev(dx, dy), device_id_type=MESH)
    pl.semaphore_wait(barrier, len(peers))

    started = []

    def remote(src, dst, ss, rs, where):
        copy = pltpu.make_async_remote_copy(
            src_ref=src, dst_ref=dst, send_sem=ss, recv_sem=rs, device_id=where, device_id_type=MESH
        )
        copy.start()
        started.append(copy)
        return copy

    def ring(k, h, d):
        block = lax.rem(y - d * (k - 1) + NY, NY)
        piece = state0.at[2 * h:2 * h + 2, block]
        i = (1 - d) // 2
        return remote(piece, piece, agy_ss.at[i, k - 1, h], agy_rs.at[i, k - 1, h], dev(0, d))

    held = {}

    def ring_round(k):
        for h in range(2):
            for d in (1, -1):
                if k > 1:
                    held[k - 1, h, d].wait_recv()
                if k < 4 or (h == 0) == (d == 1):
                    held[k, h, d] = ring(k, h, d)

    passed, crossed = {}, []

    def pass_on(j):
        passed[j] = remote(
            own_ref.at[1], state1.at[x, y], agv_ss.at[j + 3], agv_rs.at[j + 3], dev(0, j)
        )

    def cross(j):
        there = state1.at[x, lax.rem(y - j + NY, NY)]
        if j:
            passed[j].wait_recv()
        for i in (1, 3, 2):
            crossed.append(remote(
                there if j else own_ref.at[1], there, agu_ss.at[j + 3, i - 1], agu_rs.at[j + 3, i - 1], dev(i, 0)
            ))

    gx = [
        remote(own_ref.at[0], state0.at[x, y], agx_ss.at[j - 1], agx_rs.at[j - 1], dev(j, 0))
        for j in (1, 3, 2)
    ]
    for j in (1, -1, 2, -2, 3, -3, 4):
        pass_on(j)
    cross(0)
    loads[2].wait()
    for copy in gx:
        copy.wait_recv()
    ring_round(1)
    cross(1), cross(-1)
    ring_round(2)
    cross(2), cross(-2), cross(3), cross(-3)
    ring_round(3)
    cross(4)
    ring_round(4)
    loads[3].wait()
    held[4, 0, 1].wait_recv()
    held[4, 1, -1].wait_recv()

    loads[0].wait()
    rows = NX * NY * own_ref.shape[2]

    def first(q, c):
        block = (state0, state1)[c][:, :, in_ref[q]].reshape(rows, half)
        prod[q, :, c * half:(c + 1) * half] = jnp.dot(
            left[q], block, preferred_element_type=jnp.float32
        ).astype(jnp.bfloat16)

    for q in range(4):
        first(q, 0)
    for copy in crossed:
        copy.wait_recv()
    for q in range(4):
        first(q, 1)
    loads[1].wait()

    weight = [
        [
            jnp.where((out_ref[q] == t) & (q < count_ref[0]), jnp.float32(1), jnp.float32(0))
            for t in range(4)
        ]
        for q in range(4)
    ]

    def second(c, h):
        span = slice(h * (rows // 2), (h + 1) * (rows // 2))
        proj = [
            lax.dot_general(
                prod[q, span], right[q, c * half:(c + 1) * half],
                (((1,), (1,)), ((), ())), preferred_element_type=jnp.float32,
            )
            for q in range(4)
        ]
        for t in range(4):
            total = proj[0] * weight[0][t]
            for q in range(1, 4):
                total = total + proj[q] * weight[q][t]
            part[c, 2 * h:2 * h + 2, :, t] = total.reshape(2, NY, own_ref.shape[2], half)

    def scatter_y_x(c):
        got = {}

        def step(k, h, d):
            i = (1 - d) // 2
            value = part[c, 2 * h:2 * h + 2, lax.rem(y + d * k + NY, NY)]
            if (k + 1, h, d) in got:
                got[k + 1, h, d].wait_recv()
                value = value + y_recv[i, k, h].astype(jnp.float32)
            y_send[i, k - 1, h] = value.astype(jnp.bfloat16)
            got[k, h, d] = remote(
                y_send.at[i, k - 1, h], y_recv.at[i, k - 1, h],
                rsy_ss.at[i, k - 1, h], rsy_rs.at[i, k - 1, h], dev(0, d),
            )

        step(4, 0, 1), step(4, 1, -1), step(3, 1, 1), step(3, 0, -1)
        yield
        step(3, 0, 1), step(3, 1, -1)
        yield
        for k in (2, 1):
            step(k, 1, 1), step(k, 0, -1)
            yield
            step(k, 0, 1), step(k, 1, -1)
            yield
        for h in (0, 1):
            value = part[c, 2 * h:2 * h + 2, y]
            for d in (1, -1):
                got[1, h, d].wait_recv()
                value = value + y_recv[(1 - d) // 2, 0, h].astype(jnp.float32)
            fbuf[2 * h:2 * h + 2] = value
        cross = []
        for j in (2, 1, 3):
            x_send[j - 1] = fbuf[lax.rem(x + j, NX)].astype(jnp.bfloat16)
            cross.append(remote(
                x_send.at[j - 1], x_recv.at[j - 1],
                rsx_ss.at[j - 1], rsx_rs.at[j - 1], dev(j, 0),
            ))
        yield
        value = fbuf[x]
        for copy in cross:
            copy.wait_recv()
        for j in (1, 2, 3):
            value = value + x_recv[j - 1].astype(jnp.float32)
        o_ref[:, :, c * half:(c + 1) * half] = value.astype(jnp.bfloat16)

    groups = [(4, 3), (-3, 2), (-2, 1), (-1, 0)]

    def scatter_x_y(c):
        got, last = {}, []

        def block(dx, j):
            return part[c, lax.rem(x + dx, NX), lax.rem(y + j + NY, NY)]

        def spread(n):
            for i in (2, 1, 3):
                for m, j in enumerate(groups[n]):
                    u_send[n, i - 1, m] = block(i, j).astype(jnp.bfloat16)
                got[n, i] = remote(
                    u_send.at[n, i - 1], u_recv.at[n, i - 1],
                    rsu_ss.at[n, i - 1], rsu_rs.at[n, i - 1], dev(i, 0),
                )

        def settle(n):
            for i in (1, 3, 2):
                got[n, i].wait_recv()
            for m, j in enumerate(groups[n]):
                value = block(0, j)
                for i in range(3):
                    value = value + u_recv[n, i, m].astype(jnp.float32)
                if j == 0:
                    gbuf[...] = value
                else:
                    v_send[j + 3] = value.astype(jnp.bfloat16)
                    last.append((j + 3, remote(
                        v_send.at[j + 3], v_recv.at[j + 3], rsv_ss.at[j + 3], rsv_rs.at[j + 3], dev(0, j)
                    )))

        spread(0), spread(1), spread(2), spread(3)
        yield
        for n in range(4):
            settle(n)
            yield
        value = gbuf[...]
        for slot, copy in last:
            copy.wait_recv()
            value = value + v_recv[slot].astype(jnp.float32)
        o_ref[:, :, c * half:(c + 1) * half] = value.astype(jnp.bfloat16)

    second(1, 0)
    second(1, 1)
    flow0, flow1 = scatter_y_x(0), scatter_x_y(1)
    next(flow1)
    second(0, 0)
    second(0, 1)
    next(flow0)
    live = [flow0, flow1]
    while live:
        for flow in list(live):
            try:
                next(flow)
            except StopIteration:
                live.remove(flow)
    for copy in started:
        copy.wait_send()


def on_device(wavefunction, left_ops, right_ops, in_sector, out_sector, term_count):
    block, sectors, order = wavefunction.shape
    half = order // 2
    own = wavefunction.reshape(block, sectors, 2, half).transpose(2, 1, 0, 3)
    slots = left_ops.shape[0]
    piece = (sectors, block, half)
    vmem = pl.BlockSpec(memory_space=pltpu.VMEM)
    smem = pl.BlockSpec(memory_space=pltpu.SMEM)
    hbm = pl.BlockSpec(memory_space=pl.ANY)
    dma = pltpu.SemaphoreType.DMA
    result = pl.pallas_call(
        kernel,
        out_shape=jax.ShapeDtypeStruct((sectors, block, order), jnp.bfloat16),
        in_specs=[smem, smem, smem, vmem, hbm, hbm],
        out_specs=vmem,
        scratch_shapes=[
            pltpu.VMEM((NX, NY, *piece), jnp.bfloat16),
            pltpu.VMEM((NX, NY, *piece), jnp.bfloat16),
            pltpu.VMEM(left_ops.shape, jnp.bfloat16),
            pltpu.VMEM(right_ops.shape, jnp.bfloat16),
            pltpu.VMEM((slots, left_ops.shape[1], order), jnp.bfloat16),
            pltpu.VMEM((2, NX, NY, *piece), jnp.float32),
            pltpu.VMEM((NX, *piece), jnp.float32),
            pltpu.VMEM(piece, jnp.float32),
            pltpu.VMEM((2, 4, 2, 2, *piece), jnp.bfloat16),
            pltpu.VMEM((2, 4, 2, 2, *piece), jnp.bfloat16),
            pltpu.VMEM((3, *piece), jnp.bfloat16),
            pltpu.VMEM((3, *piece), jnp.bfloat16),
            pltpu.VMEM((8, *piece), jnp.bfloat16),
            pltpu.VMEM((8, *piece), jnp.bfloat16),
            pltpu.VMEM((4, 3, 2, *piece), jnp.bfloat16),
            pltpu.VMEM((4, 3, 2, *piece), jnp.bfloat16),
            dma((4,)),
            dma((3,)), dma((3,)),
            dma((2, 4, 2)), dma((2, 4, 2)),
            dma((8,)), dma((8,)),
            dma((8, 3)), dma((8, 3)),
            dma((2, 4, 2)), dma((2, 4, 2)),
            dma((3,)), dma((3,)),
            dma((8,)), dma((8,)),
            dma((4, 3)), dma((4, 3)),
        ],
        compiler_params=pltpu.CompilerParams(collective_id=0, has_side_effects=True),
        name="gather_apply_scatter",
    )(in_sector, out_sector, term_count, own, left_ops, right_ops)
    return result.transpose(1, 0, 2)


def solution(mesh):
    return jax.shard_map(
        on_device,
        mesh=mesh,
        in_specs=(
            P("grp", "sec", None),
            P(("grp", "sec"), None, None),
            P(("grp", "sec"), None, None),
            P(("grp", "sec")),
            P(("grp", "sec")),
            P(("grp", "sec")),
        ),
        out_specs=P("grp", "sec", None),
        check_vma=False,
    )
```

```python
import jax
import jax.numpy as jnp
from jax import lax
from jax.experimental import pallas as pl
from jax.experimental.pallas import tpu as pltpu
from jax.sharding import PartitionSpec as P

NX, NY = 4, 8
MESH = pl.DeviceIdType.MESH


def kernel(
    in_ref, out_ref, count_ref, wave_ref, left_hbm, right_hbm, o_ref,
    own_ref, state0, state1, left, right, prod, part, fbuf, gbuf,
    y_send, y_recv, x_send, x_recv, v_send, v_recv, u_send, u_recv,
    load_sem, agx_ss, agx_rs, agy_ss, agy_rs, agv_ss, agv_rs, agu_ss, agu_rs,
    rsy_ss, rsy_rs, rsx_ss, rsx_rs, rsv_ss, rsv_rs, rsu_ss, rsu_rs,
):
    g = lax.axis_index("grp")
    x, y = g // NY, lax.rem(g, NY)
    half = o_ref.shape[2] // 2

    def dev(dx, dy):
        return {"grp": lax.rem(x + dx + NX, NX) * NY + lax.rem(y + dy + NY, NY)}

    block = wave_ref[...].astype(jnp.float32)
    for s in range(block.shape[1]):
        for c in range(2):
            own_ref[c, s] = block[:, s, c * half:(c + 1) * half].astype(jnp.bfloat16)

    loads = [
        pltpu.make_async_copy(left_hbm, left, load_sem.at[0]),
        pltpu.make_async_copy(right_hbm, right, load_sem.at[1]),
        pltpu.make_async_copy(own_ref.at[0], state0.at[x, y], load_sem.at[2]),
        pltpu.make_async_copy(own_ref.at[1], state1.at[x, y], load_sem.at[3]),
    ]
    for load in loads:
        load.start()

    barrier = pltpu.get_barrier_semaphore()
    peers = [(j, 0) for j in range(1, NX)] + [(0, j) for j in range(1, NY)]
    for dx, dy in peers:
        pl.semaphore_signal(barrier, inc=1, device_id=dev(dx, dy), device_id_type=MESH)
    pl.semaphore_wait(barrier, len(peers))

    started, done = [], {}

    def remote(src, dst, ss, rs, where):
        copy = pltpu.make_async_remote_copy(
            src_ref=src, dst_ref=dst, send_sem=ss, recv_sem=rs, device_id=where, device_id_type=MESH
        )
        copy.start()
        started.append(copy)
        return copy

    def ring(k, h, d):
        block = lax.rem(y - d * (k - 1) + NY, NY)
        piece = state0.at[2 * h:2 * h + 2, block]
        i = (1 - d) // 2
        return remote(piece, piece, agy_ss.at[i, k - 1, h], agy_rs.at[i, k - 1, h], dev(0, d))

    held = {}

    def ring_round(k):
        for h in range(2):
            for d in (1, -1):
                if k > 1:
                    held[k - 1, h, d].wait_recv()
                if k < 4 or (h == 0) == (d == 1):
                    held[k, h, d] = ring(k, h, d)

    passed, crossed = {}, []

    def pass_on(j):
        passed[j] = remote(
            own_ref.at[1], state1.at[x, y], agv_ss.at[j + 3], agv_rs.at[j + 3], dev(0, j)
        )

    def cross(j):
        there = state1.at[x, lax.rem(y - j + NY, NY)]
        if j:
            passed[j].wait_recv()
        for i in (1, 3, 2):
            crossed.append(remote(
                there if j else own_ref.at[1], there, agu_ss.at[j + 3, i - 1], agu_rs.at[j + 3, i - 1], dev(i, 0)
            ))

    gx = [
        remote(own_ref.at[0], state0.at[x, y], agx_ss.at[j - 1], agx_rs.at[j - 1], dev(j, 0))
        for j in (1, 3, 2)
    ]
    for j in (1, -1, 2, -2, 3, -3, 4):
        pass_on(j)
    cross(0)
    loads[2].wait()
    for copy in gx:
        copy.wait_recv()
    ring_round(1)
    cross(1), cross(-1)
    ring_round(2)
    cross(2), cross(-2), cross(3), cross(-3)
    ring_round(3)
    cross(4)
    ring_round(4)
    loads[3].wait()
    held[4, 0, 1].wait_recv()
    held[4, 1, -1].wait_recv()

    loads[0].wait()
    rows = NX * NY * own_ref.shape[2]

    def first(q, c):
        block = (state0, state1)[c][:, :, in_ref[q]].reshape(rows, half)
        prod[q, :, c * half:(c + 1) * half] = jnp.dot(
            left[q], block, preferred_element_type=jnp.float32
        ).astype(jnp.bfloat16)

    for q in range(4):
        first(q, 0)
    for copy in crossed:
        copy.wait_recv()
    for q in range(4):
        first(q, 1)
    loads[1].wait()

    weight = [
        [
            jnp.where((out_ref[q] == t) & (q < count_ref[0]), jnp.float32(1), jnp.float32(0))
            for t in range(4)
        ]
        for q in range(4)
    ]

    def second(c, h):
        span = slice(h * (rows // 2), (h + 1) * (rows // 2))
        proj = [
            lax.dot_general(
                prod[q, span], right[q, c * half:(c + 1) * half],
                (((1,), (1,)), ((), ())), preferred_element_type=jnp.float32,
            )
            for q in range(4)
        ]
        for t in range(4):
            total = proj[0] * weight[0][t]
            for q in range(1, 4):
                total = total + proj[q] * weight[q][t]
            part[c, 2 * h:2 * h + 2, :, t] = total.reshape(2, NY, own_ref.shape[2], half)

    def scatter_y_x(c):
        got = {}

        def step(k, h, d):
            i = (1 - d) // 2
            value = part[c, 2 * h:2 * h + 2, lax.rem(y + d * k + NY, NY)]
            if (k + 1, h, d) in got:
                got[k + 1, h, d].wait_recv()
                value = value + y_recv[i, k, h].astype(jnp.float32)
            y_send[i, k - 1, h] = value.astype(jnp.bfloat16)
            got[k, h, d] = remote(
                y_send.at[i, k - 1, h], y_recv.at[i, k - 1, h],
                rsy_ss.at[i, k - 1, h], rsy_rs.at[i, k - 1, h], dev(0, d),
            )

        step(4, 0, 1), step(4, 1, -1), step(3, 1, 1), step(3, 0, -1)
        yield
        step(3, 0, 1), step(3, 1, -1)
        yield
        for k in (2, 1):
            step(k, 1, 1), step(k, 0, -1)
            yield
            step(k, 0, 1), step(k, 1, -1)
            yield
        for h in (0, 1):
            value = part[c, 2 * h:2 * h + 2, y]
            for d in (1, -1):
                got[1, h, d].wait_recv()
                value = value + y_recv[(1 - d) // 2, 0, h].astype(jnp.float32)
            fbuf[2 * h:2 * h + 2] = value
        cross = []
        for j in (2, 1, 3):
            x_send[j - 1] = fbuf[lax.rem(x + j, NX)].astype(jnp.bfloat16)
            cross.append(remote(
                x_send.at[j - 1], x_recv.at[j - 1],
                rsx_ss.at[j - 1], rsx_rs.at[j - 1], dev(j, 0),
            ))
        yield
        value = fbuf[x]
        for copy in cross:
            copy.wait_recv()
        for j in (1, 2, 3):
            value = value + x_recv[j - 1].astype(jnp.float32)
        done[c] = value

    groups = [(4, 3), (-3, 2), (-2, 1), (-1, 0)]

    def scatter_x_y(c):
        got, last = {}, []

        def block(dx, j):
            return part[c, lax.rem(x + dx, NX), lax.rem(y + j + NY, NY)]

        def spread(n):
            for i in (2, 1, 3):
                for m, j in enumerate(groups[n]):
                    u_send[n, i - 1, m] = block(i, j).astype(jnp.bfloat16)
                got[n, i] = remote(
                    u_send.at[n, i - 1], u_recv.at[n, i - 1],
                    rsu_ss.at[n, i - 1], rsu_rs.at[n, i - 1], dev(i, 0),
                )

        def settle(n):
            for i in (1, 3, 2):
                got[n, i].wait_recv()
            for m, j in enumerate(groups[n]):
                value = block(0, j)
                for i in range(3):
                    value = value + u_recv[n, i, m].astype(jnp.float32)
                if j == 0:
                    gbuf[...] = value
                else:
                    v_send[j + 3] = value.astype(jnp.bfloat16)
                    last.append((j + 3, remote(
                        v_send.at[j + 3], v_recv.at[j + 3], rsv_ss.at[j + 3], rsv_rs.at[j + 3], dev(0, j)
                    )))

        spread(0), spread(1), spread(2), spread(3)
        yield
        for n in range(4):
            settle(n)
            yield
        value = gbuf[...]
        for slot, copy in last:
            copy.wait_recv()
            value = value + v_recv[slot].astype(jnp.float32)
        done[c] = value

    second(1, 0)
    second(1, 1)
    flow0, flow1 = scatter_y_x(0), scatter_x_y(1)
    next(flow1)
    second(0, 0)
    second(0, 1)
    next(flow0)
    live = [flow0, flow1]
    while live:
        for flow in list(live):
            try:
                next(flow)
            except StopIteration:
                live.remove(flow)
    o_ref[...] = jnp.swapaxes(jnp.concatenate([done[0], done[1]], axis=2), 0, 1).astype(jnp.bfloat16)
    for copy in started:
        copy.wait_send()


def on_device(wavefunction, left_ops, right_ops, in_sector, out_sector, term_count):
    block, sectors, order = wavefunction.shape
    half = order // 2
    slots = left_ops.shape[0]
    piece = (sectors, block, half)
    vmem = pl.BlockSpec(memory_space=pltpu.VMEM)
    smem = pl.BlockSpec(memory_space=pltpu.SMEM)
    hbm = pl.BlockSpec(memory_space=pl.ANY)
    dma = pltpu.SemaphoreType.DMA
    return pl.pallas_call(
        kernel,
        out_shape=jax.ShapeDtypeStruct(wavefunction.shape, jnp.bfloat16),
        in_specs=[smem, smem, smem, vmem, hbm, hbm],
        out_specs=vmem,
        scratch_shapes=[
            pltpu.VMEM((2, *piece), jnp.bfloat16),
            pltpu.VMEM((NX, NY, *piece), jnp.bfloat16),
            pltpu.VMEM((NX, NY, *piece), jnp.bfloat16),
            pltpu.VMEM(left_ops.shape, jnp.bfloat16),
            pltpu.VMEM(right_ops.shape, jnp.bfloat16),
            pltpu.VMEM((slots, left_ops.shape[1], order), jnp.bfloat16),
            pltpu.VMEM((2, NX, NY, *piece), jnp.float32),
            pltpu.VMEM((NX, *piece), jnp.float32),
            pltpu.VMEM(piece, jnp.float32),
            pltpu.VMEM((2, 4, 2, 2, *piece), jnp.bfloat16),
            pltpu.VMEM((2, 4, 2, 2, *piece), jnp.bfloat16),
            pltpu.VMEM((3, *piece), jnp.bfloat16),
            pltpu.VMEM((3, *piece), jnp.bfloat16),
            pltpu.VMEM((8, *piece), jnp.bfloat16),
            pltpu.VMEM((8, *piece), jnp.bfloat16),
            pltpu.VMEM((4, 3, 2, *piece), jnp.bfloat16),
            pltpu.VMEM((4, 3, 2, *piece), jnp.bfloat16),
            dma((4,)),
            dma((3,)), dma((3,)),
            dma((2, 4, 2)), dma((2, 4, 2)),
            dma((8,)), dma((8,)),
            dma((8, 3)), dma((8, 3)),
            dma((2, 4, 2)), dma((2, 4, 2)),
            dma((3,)), dma((3,)),
            dma((8,)), dma((8,)),
            dma((4, 3)), dma((4, 3)),
        ],
        compiler_params=pltpu.CompilerParams(collective_id=0, has_side_effects=True),
        name="gather_apply_scatter",
    )(in_sector, out_sector, term_count, wavefunction, left_ops, right_ops)


def solution(mesh):
    return jax.shard_map(
        on_device,
        mesh=mesh,
        in_specs=(
            P("grp", "sec", None),
            P(("grp", "sec"), None, None),
            P(("grp", "sec"), None, None),
            P(("grp", "sec")),
            P(("grp", "sec")),
            P(("grp", "sec")),
        ),
        out_specs=P("grp", "sec", None),
        check_vma=False,
    )
```
